32 devices in a mesh: sec: 4 (over y, core), row: 2 (over x), col: 4 (over z).
Axes of the slice: x: 2, y: 2, z: 4, core: 2. Of those that a mesh axis runs over, the one named last changes fastest.
Arguments:
- child_inv: bfloat16 [4, 4096, 4096], P('sec', 'col', 'row'), as said below
- child_low: bfloat16 [4, 2048, 4096], P('sec', 'row', 'col'), may hold values from -0.09375 to 0.09375
- parent_inv: bfloat16 [4, 6144, 3072], P('sec', 'col', 'row'), as said below
- parent_low: bfloat16 [4, 2048, 3072], P('sec', 'row', 'col'), may hold values from -0.078125 to 0.078125
- root_inv: bfloat16 [12288, 12288], P('col', ('sec', 'row')), as said below
- child_map: int32 [4, 2048], replicated, may hold values from 0 to 8191, as said below
- parent_map: int32 [2, 2048], replicated, may hold values from 0 to 12287, as said below
- child_rhs: float32 [4, 4096, 512], P('sec', 'row', 'col'), may hold values from -6 to 6
- parent_rhs: float32 [4, 3072, 512], P('sec', 'row', 'col'), may hold values from -6 to 6
- root_rhs: float32 [12288, 512], P(('sec', 'row'), 'col'), may hold values from -6 to 6
- child_back: float32 [4, 4096, 512], P('sec', 'col', 'row'), may hold values from -6 to 6
- parent_back: float32 [4, 3072, 512], P('sec', 'col', 'row'), may hold values from -6 to 6
- root_back: float32 [4, 3072, 512], P('col', ('sec', 'row')), may hold values from -6 to 6
Outputs:
- child_up: float32 [4, 4096, 512], P('sec', 'col', 'row')
- parent_up: float32 [4, 3072, 512], P('sec', 'col', 'row')
- root_up: float32 [4, 3072, 512], P('col', ('sec', 'row'))
- child_x: float32 [4, 4096, 512], P('sec', 'row', 'col')
- parent_x: float32 [4, 3072, 512], P('sec', 'row', 'col')
- root_x: float32 [12288, 512], P(('sec', 'row'), 'col')
The draws below stay inside these ranges and needn't reach their ends.
Inputs may be any that keep to these rules, and one draw needn't show every extreme that they name: `child_inv`: zero above the diagonal of each child pivot block. `parent_inv`: the two halves side by side are zero above the diagonal. `root_inv`: zero above the diagonal. `child_map`: entries of one row are distinct; row s points into the front of parent s // 2. `parent_map`: entries of one row are distinct.
All inputs are finite; a program needn't handle non-finite values.
Results may differ from the reference program's by a relative error of at most 0.014.
Values may be sent and summed in bfloat16 or wider, within the bound.
No kernel may reach another device: no remote copies, remote signals or barrier semaphores. Data moves between devices by JAX's collectives and lax.ppermute only.
A program may use at most 128 MiB of HBM per device.

```python
import jax
import jax.numpy as jnp

P1 = 4096
C1 = 2048
P2 = 6144
C2 = 2048
P3 = 12288
FW = 512
BW = 512
SECTIONS = 4
COL_BLOCKS = 4
N_COL = 4


def lower_factor(key, members, order):
    base = jax.random.normal(key, (members, order, order), jnp.float32)
    return jnp.tril(base) / jnp.sqrt(order * 1.0) + jnp.eye(order, dtype=jnp.float32)


def spread_map(key, members, length, extent):
    result_rows = []
    for member in range(members):
        member_key = jax.random.fold_in(key, member)
        middle = jax.random.permutation(jax.random.fold_in(member_key, 1), extent - 2)[:length - 2] + 1
        picked = jnp.concatenate([jnp.array([0, extent - 1], jnp.int32), middle.astype(jnp.int32)])
        result_rows.append(jax.random.permutation(jax.random.fold_in(member_key, 2), picked))
    return jnp.stack(result_rows).astype(jnp.int32)


def draw_child_inv(key, part):
    return lower_factor(jax.random.fold_in(key, 11), SECTIONS, P1).astype(jnp.bfloat16)


def draw_parent_inv(key, part):
    whole = lower_factor(jax.random.fold_in(key, 12), 2, P2)
    return whole.reshape(2, P2, 2, P2 // 2).transpose(0, 2, 1, 3).reshape(4, P2, P2 // 2).astype(jnp.bfloat16)


def draw_root_inv(key, part):
    return lower_factor(jax.random.fold_in(key, 13), 1, P3)[0].astype(jnp.bfloat16)


def draw_child_map(key, part):
    return spread_map(jax.random.fold_in(key, 21), SECTIONS, C1, P2 + C2)


def draw_parent_map(key, part):
    return spread_map(jax.random.fold_in(key, 22), 2, C2, P3)


def level_of(rng, shape, shards, smallest, high):
    gain = 1.0
    for position, parts in shards:
        heights = jax.random.uniform(jax.random.fold_in(jax.random.fold_in(rng, 6), position), (parts,), jnp.float32, smallest / len(shards), high / len(shards))
        gain = gain * jnp.repeat(jnp.exp(heights), shape[position] // parts).reshape((-1,) + (1,) * (len(shape) - 1 - position))
    return gain


def gaussian(rng, shape, scale, limit, shards=(), held_as=jnp.bfloat16):
    gain = level_of(rng, shape, shards, -0.22, 0.18) if shards else 1.0
    values = jax.random.normal(rng, shape, jnp.float32) * scale * gain
    return jnp.minimum(jnp.maximum(values, -limit), limit).astype(held_as)


def setup_inputs(seed: int = 0) -> dict:
    key_of = jax.random.split(jax.random.key(seed), 14)
    return {
        "child_inv": draw_child_inv(jax.random.fold_in(key_of[13], 71), 0),
        "child_low": gaussian(key_of[1], (SECTIONS, C1, P1), P1 ** -0.5, 0.09375, ((0, 4), (1, 2), (2, 4))),
        "parent_inv": draw_parent_inv(jax.random.fold_in(key_of[13], 71), 0),
        "parent_low": gaussian(key_of[3], (SECTIONS, C2, P2 // 2), P2 ** -0.5, 0.078125, ((0, 4), (1, 2), (2, 4))),
        "root_inv": draw_root_inv(jax.random.fold_in(key_of[13], 71), 0),
        "child_map": draw_child_map(jax.random.fold_in(key_of[13], 71), 0),
        "parent_map": draw_parent_map(jax.random.fold_in(key_of[13], 71), 0),
        "child_rhs": gaussian(key_of[7], (SECTIONS, P1, FW), 1.0, 6.0, ((0, 4), (1, 2), (2, 4)), jnp.float32),
        "parent_rhs": gaussian(key_of[8], (SECTIONS, P2 // 2, FW), 1.0, 6.0, ((0, 4), (1, 2), (2, 4)), jnp.float32),
        "root_rhs": gaussian(key_of[9], (P3, FW), 1.0, 6.0, ((0, 8), (1, 4)), jnp.float32),
        "child_back": gaussian(key_of[10], (SECTIONS, P1, BW), 1.0, 6.0, ((0, 4), (1, 4), (2, 2)), jnp.float32),
        "parent_back": gaussian(key_of[11], (SECTIONS, P2 // 2, BW), 1.0, 6.0, ((0, 4), (1, 4), (2, 2)), jnp.float32),
        "root_back": gaussian(key_of[12], (COL_BLOCKS, P3 // COL_BLOCKS, BW), 1.0, 6.0, ((0, 4), (1, 8)), jnp.float32),
    }


def product(left, right):
    return jnp.dot(left, right.astype(jnp.bfloat16), preferred_element_type=jnp.float32)


def reference(child_inv, child_low, parent_inv, parent_low, root_inv, child_map, parent_map, child_rhs, parent_rhs, root_rhs, child_back, parent_back, root_back):
    quota = P2 // (2 * N_COL)
    child_up = jnp.stack([product(child_inv[member], child_rhs[member]) for member in range(4)])
    contrib = [-product(child_low[member], child_up[member]) for member in range(4)]
    pivot_rhs = parent_rhs.reshape(2, P2, FW)
    pivot_back = parent_back.reshape(2, 2, N_COL, quota, BW).transpose(0, 2, 1, 3, 4).reshape(2, P2, BW)
    inverses = []
    couplings = []
    solved = []
    updates = []
    for parent in range(2):
        inverse = jnp.concatenate([parent_inv[2 * parent], parent_inv[2 * parent + 1]], axis=1)
        coupling = parent_low[2 * parent:2 * parent + 2].reshape(2, C2, N_COL, quota).transpose(1, 2, 0, 3).reshape(C2, P2)
        front = jnp.zeros((P2 + C2, FW), jnp.float32)
        front = front.at[child_map[2 * parent]].add(contrib[2 * parent])
        front = front.at[child_map[2 * parent + 1]].add(contrib[2 * parent + 1])
        upward = product(inverse, pivot_rhs[parent] + front[:P2])
        updates.append(front[P2:] - product(coupling, upward))
        inverses.append(inverse)
        couplings.append(coupling)
        solved.append(upward)
    parent_up = jnp.stack(solved).reshape(2, N_COL, 2, quota, FW).transpose(0, 2, 1, 3, 4).reshape(4, P2 // 2, FW)
    root_front = jnp.zeros((P3, FW), jnp.float32)
    root_front = root_front.at[parent_map[0]].add(updates[0])
    root_front = root_front.at[parent_map[1]].add(updates[1])
    root_up = product(root_inv, root_rhs + root_front).reshape(N_COL, P3 // N_COL, FW)
    root_x = product(root_inv.T, root_back.reshape(P3, BW))
    root_bf = root_x.astype(jnp.bfloat16)
    parent_rows = []
    fronts = []
    for parent in range(2):
        picked = root_bf[parent_map[parent]]
        residue = pivot_back[parent] - jnp.dot(couplings[parent].T, picked, preferred_element_type=jnp.float32)
        solution = product(inverses[parent].T, residue)
        parent_rows.append(solution)
        fronts.append(jnp.concatenate([solution.astype(jnp.bfloat16), picked], axis=0))
    parent_x = jnp.stack(parent_rows).reshape(4, P2 // 2, BW)
    child_rows = []
    for member in range(4):
        chosen = fronts[member // 2][child_map[member]]
        residue = child_back[member] - jnp.dot(child_low[member].T, chosen, preferred_element_type=jnp.float32)
        child_rows.append(product(child_inv[member].T, residue))
    child_x = jnp.stack(child_rows)
    return child_up, parent_up, root_up, child_x, parent_x, root_x
```

```python
import jax
import jax.numpy as jnp
from jax import lax
from jax.sharding import PartitionSpec as P

BF = jnp.bfloat16
F32 = jnp.float32


def swap(x, axis, mask):
    return lax.ppermute(x, axis, [(i, i ^ mask) for i in range(lax.axis_size(axis))])


def spread_cols(block):
    return lax.all_gather(block, "col", axis=1, tiled=True)


def sum_cols(block):
    return lax.psum_scatter(block.astype(BF), "col", scatter_dimension=1, tiled=True).astype(F32)


def matmul(left, right):
    return jnp.dot(left, right, preferred_element_type=F32)


def matmul_t(left, right):
    return lax.dot_general(left, right, (((0,), (0,)), ((), ())), preferred_element_type=F32)


def row_total(part):
    if lax.axis_size("row") == 2:
        return part + swap(part.astype(BF), "row", 1).astype(F32)
    share = lax.psum_scatter(part.astype(BF), "row", scatter_dimension=1, tiled=True)
    return lax.all_gather(share, "row", axis=1, tiled=True).astype(F32)


def row_ids():
    n_row = lax.axis_size("row")
    if n_row == 2:
        me = lax.axis_index("row")
        return jnp.stack([me, 1 - me])
    return jnp.arange(n_row, dtype=jnp.int32)


def row_gather(block):
    if lax.axis_size("row") == 2:
        return jnp.concatenate([block, swap(block, "row", 1)], 0)
    return lax.all_gather(block, "row", axis=0, tiled=True)


def row_scatter(part):
    if lax.axis_size("row") == 2:
        amount = part.shape[0] // 2
        return part[:amount] + swap(part[amount:], "row", 1)
    return lax.psum_scatter(part, "row", scatter_dimension=0, tiled=True)


def far_masks():
    masks = []
    mask = 2
    while mask < lax.axis_size("sec"):
        masks.append(mask)
        mask *= 2
    return masks


def place_ids():
    sections = [lax.axis_index("sec")]
    for mask in far_masks():
        sections = sections + [s ^ mask for s in sections]
    sections = sections + [s ^ 1 for s in sections]
    rows = row_ids()
    return jnp.concatenate([s * rows.shape[0] + rows for s in sections])


def place_gather(block):
    blocks = [block]
    for mask in far_masks():
        blocks = blocks + [swap(b, "sec", mask) for b in blocks]
    near = jnp.concatenate([row_gather(b) for b in blocks], 0)
    return jnp.concatenate([near, swap(near, "sec", 1)], 0)


def place_scatter(near, away):
    part = near + swap(away, "sec", 1)
    for mask in reversed(far_masks()):
        amount = part.shape[0] // 2
        part = part[:amount] + swap(part[amount:], "sec", mask)
    return row_scatter(part)


def one_hot(rows, cols):
    return (rows[:, None] == cols[None, :]).astype(BF)


def take_part(block, index, count, axis):
    size = block.shape[axis] // count
    return lax.dynamic_slice_in_dim(block, index * size, size, axis)


def wide(block, index, count):
    parts = [jnp.where(index == i, block, 0.0) for i in range(count)]
    return jnp.concatenate(parts, 1)


def per_device(
    child_inv,
    child_low,
    parent_inv,
    parent_low,
    root_inv,
    child_map,
    parent_map,
    child_rhs,
    parent_rhs,
    root_rhs,
    child_back,
    parent_back,
    root_back,
):
    n_row = lax.axis_size("row")
    n_sec = lax.axis_size("sec")
    n_col = lax.axis_size("col")
    section = lax.axis_index("sec")
    row_id = lax.axis_index("row")
    side = section % 2
    c1 = child_map.shape[1]
    c2 = parent_map.shape[1]
    p2 = parent_inv.shape[1] * n_col
    pivot_rows = p2 // (2 * n_row)
    cont_rows = c2 // (2 * n_row)
    stride = pivot_rows + cont_rows
    root_block = root_rhs.shape[0]

    own_map = lax.dynamic_index_in_dim(child_map, section, 0, False)
    other_map = lax.dynamic_index_in_dim(child_map, section ^ 1, 0, False)
    rows = row_ids()
    targets = jnp.concatenate(
        [m.reshape(n_row, c1 // n_row)[rows].reshape(-1) for m in (own_map, other_map)]
    )
    offset = targets - p2
    own_block = side * n_row + row_id
    pivot_local = targets - own_block * pivot_rows
    pivot_slot = jnp.where((pivot_local >= 0) & (pivot_local < pivot_rows), pivot_local, -1)
    cont_local = offset - (row_id * 2 + side) * cont_rows
    cont_slot = jnp.where(
        (cont_local >= 0) & (cont_local < cont_rows), cont_local + pivot_rows, -1
    )
    slots = jnp.where(targets < p2, pivot_slot, cont_slot)
    front_ids = jnp.arange(stride, dtype=jnp.int32)

    place = section * n_row + row_id
    by_place = parent_map.reshape(n_sec // 2, n_row, 2, cont_rows).transpose(0, 2, 1, 3)
    root_slots = by_place.reshape(n_sec * n_row, cont_rows)[place_ids()].reshape(-1)
    root_slots = root_slots - place * root_block
    root_ids = jnp.arange(root_block, dtype=jnp.int32)

    part = matmul(child_inv[0], spread_cols(child_rhs[0].astype(BF)))
    child_total = row_total(part)
    child_up = take_part(child_total, row_id, n_row, 1)
    lowered = sum_cols(matmul(child_low[0], child_total.astype(BF))).astype(BF)
    near = row_gather(lowered)
    both = jnp.concatenate([near, swap(near, "sec", 1)], 0)
    front = -matmul(one_hot(front_ids, slots), both)

    back_wide = lax.all_gather(root_back[0].astype(BF), ("sec", "row"), axis=0, tiled=True)
    root_x = sum_cols(matmul_t(root_inv, back_wide))
    root_sel = matmul(one_hot(root_slots, root_ids), root_x.astype(BF)).astype(BF)
    half = root_sel.shape[0] // 2
    picked = place_scatter(root_sel[:half], root_sel[half:])

    pivot_in = parent_rhs[0] + front[:pivot_rows]
    share = matmul(parent_inv[0], spread_cols(pivot_in.astype(BF)))
    keep = take_part(share, side, 2, 0)
    away = take_part(share, side ^ 1, 2, 0).astype(BF)
    parent_total = row_total(keep + swap(away, "sec", 1).astype(F32))
    parent_up = take_part(parent_total, row_id, n_row, 1)
    update = matmul(parent_low[0], parent_total.astype(BF))
    keep = take_part(update, side, 2, 0)
    away = take_part(update, side ^ 1, 2, 0).astype(BF)
    update = sum_cols(keep + swap(away, "sec", 1).astype(F32))
    contrib = front[pivot_rows:] - update

    mine = spread_cols(picked)
    other = swap(mine, "sec", 1)
    low = parent_low[0]
    taken = matmul_t(take_part(low, side, 2, 0), mine) + matmul_t(
        take_part(low, side ^ 1, 2, 0), other
    )
    residue = row_total(wide(parent_back[0], row_id, n_row) - taken).astype(BF)
    far = swap(residue, "sec", 1)
    inv = parent_inv[0]
    parent_x = sum_cols(
        matmul_t(take_part(inv, side, 2, 0), residue)
        + matmul_t(take_part(inv, side ^ 1, 2, 0), far)
    )

    every = place_gather(contrib.astype(BF))
    root_in = root_rhs + matmul(one_hot(root_ids, root_slots), every)
    root_part = matmul(root_inv, spread_cols(root_in.astype(BF)))
    root_up = lax.psum_scatter(
        root_part.astype(BF), ("sec", "row"), scatter_dimension=0, tiled=True
    ).astype(F32)

    front_x = jnp.concatenate([parent_x.astype(BF), picked], 0)
    chosen = matmul(one_hot(slots, front_ids), front_x).astype(BF)
    chosen = row_scatter(chosen[:c1] + swap(chosen[c1:], "sec", 1))
    taken = matmul_t(child_low[0], spread_cols(chosen))
    residue = row_total(wide(child_back[0], row_id, n_row) - taken)
    child_x = sum_cols(matmul_t(child_inv[0], residue.astype(BF)))
    return (child_up[None], parent_up[None], root_up[None], child_x[None], parent_x[None], root_x)


def solution(mesh):
    return jax.shard_map(
        per_device,
        mesh=mesh,
        in_specs=(
            P("sec", "col", "row"),
            P("sec", "row", "col"),
            P("sec", "col", "row"),
            P("sec", "row", "col"),
            P("col", ("sec", "row")),
            P(),
            P(),
            P("sec", "row", "col"),
            P("sec", "row", "col"),
            P(("sec", "row"), "col"),
            P("sec", "col", "row"),
            P("sec", "col", "row"),
            P("col", ("sec", "row"), None),
        ),
        out_specs=(
            P("sec", "col", "row"),
            P("sec", "col", "row"),
            P("col", ("sec", "row"), None),
            P("sec", "row", "col"),
            P("sec", "row", "col"),
            P(("sec", "row"), "col"),
        ),
        check_vma=False,
    )
```
